32 devices in a mesh: row: 8 (over z, x), col: 4 (over y, core).
Axes of the slice: x: 2, y: 2, z: 4, core: 2. Of those that a mesh axis runs over, the one named last changes fastest.
Arguments:
- data: bfloat16 [64, 640, 3072], P('row', None, 'col')
- slot_of_block: int32 [64], replicated, may hold values from 0 to 63, as said below
- pair_rows: int32 [8, 4], replicated, may hold values from 0 to 63, as said below
- partners: int32 [8, 4, 2], replicated, may hold values from 0 to 63, as said below
Outputs:
- ntk_tiles: float32 [8, 4, 2, 640, 640], P('row', 'col')
The draws below stay inside these ranges and needn't reach their ends.
Inputs may be any that keep to these rules, and one draw needn't show every extreme that they name: `slot_of_block`: a permutation of the blocks. `pair_rows`: the row block of device (r, c) is stored at a slot s with s // 8 == r. A partner differs from its row block; of the 2 partners of all devices with one index of row, at most 2 are stored on any one index of row (slot // 8), and some index of row stores exactly 2 of them.
All inputs are finite; a program needn't handle non-finite values.
Results may differ from the reference program's by a relative error of at most 0.0003.
Values may be sent and summed in bfloat16 or wider, within the bound.
No kernel may reach another device: no remote copies, remote signals or barrier semaphores. Data moves between devices by JAX's collectives and lax.ppermute only.
A program may use at most 128 MiB of HBM per device.

```python
import jax
import jax.numpy as jnp
from jax import lax

D = 3072
BLK = 640
BPR = 8
LAYERS = 10
CAP = 2
PAIRS_DEV = 2
NBLK = 64
N_ROW = 8
N_COL = 4


def layout(key):
    keys = jax.random.split(jax.random.fold_in(key, 7), 4)
    total = BPR * N_ROW
    slot_of_block = jax.random.permutation(keys[0], total).astype(jnp.int32)
    block_at_slot = jnp.argsort(slot_of_block).astype(jnp.int32)
    row_local = jax.random.randint(keys[1], (N_ROW, N_COL), 0, BPR)
    row_ids = jnp.arange(N_ROW, dtype=jnp.int32)[:, None]
    pair_rows = block_at_slot[row_ids * BPR + row_local]
    requests = PAIRS_DEV * N_COL
    pool = jnp.repeat(jnp.arange(N_ROW, dtype=jnp.int32), CAP)

    def one_group(group_key):
        sub = jax.random.split(group_key, 3)
        hottest = jax.random.randint(sub[0], (), 0, N_ROW)
        score = jnp.where(pool == hottest, N_ROW * CAP, 0) + jax.random.permutation(sub[1], N_ROW * CAP)
        others = pool[jnp.argsort(score)][:requests - CAP]
        owners = jnp.concatenate([jnp.full((CAP,), hottest, jnp.int32), others])
        return owners[jax.random.permutation(sub[2], requests)]
    owners = jax.vmap(one_group)(jax.random.split(keys[2], N_ROW))
    within = jax.random.randint(keys[3], (N_ROW, requests), 0, BPR)
    row_within = jnp.repeat(row_local, PAIRS_DEV, axis=1)
    within = jnp.where((owners == row_ids) & (within == row_within), (within + 1) % BPR, within)
    partners = block_at_slot[owners * BPR + within].reshape(N_ROW, N_COL, PAIRS_DEV)
    return (slot_of_block, pair_rows.astype(jnp.int32), partners.astype(jnp.int32))


def draw_slot_of_block(key, part):
    return layout(key)[0]


def draw_pair_rows(key, part):
    return layout(key)[1]


def draw_partners(key, part):
    return layout(key)[2]


def draw_data(key, part):
    keys = jax.random.split(jax.random.fold_in(key, 11), 2)
    position = jnp.arange(D, dtype=jnp.float32) / (D - 1)
    raw = jax.random.normal(keys[0], (NBLK, BLK, D), jnp.float32)
    column_scale = 3.0 ** (0.5 * position)
    row_scale = jnp.exp(jax.random.uniform(keys[1], (NBLK, BLK, 1), jnp.float32, jnp.log(0.5), jnp.log(5.0)))
    values = raw * column_scale[None, None, :] * row_scale * 0.6
    return values.astype(jnp.bfloat16)


def setup_inputs(seed: int = 0) -> dict:
    splits = jax.random.split(jax.random.key(seed), 5)
    return {
        "data": draw_data(jax.random.fold_in(splits[4], 71), 0),
        "slot_of_block": draw_slot_of_block(jax.random.fold_in(splits[4], 71), 0),
        "pair_rows": draw_pair_rows(jax.random.fold_in(splits[4], 71), 0),
        "partners": draw_partners(jax.random.fold_in(splits[4], 71), 0),
    }


weight_var = 2.0
bias_var = 0.05

def recurse(base_kernel, q_rows, q_parts):

    def one_layer(depth, carry):
        covariance, tangent, row_var, part_var = carry
        slack = jnp.maximum(row_var * part_var - covariance * covariance, 0.0)
        sine_part = jnp.sqrt(slack)
        opening = jnp.arctan2(sine_part, covariance)
        fresh = weight_var / (2.0 * jnp.pi) * (sine_part + (jnp.pi - opening) * covariance) + bias_var
        derivative = weight_var / (2.0 * jnp.pi) * (jnp.pi - opening)
        tangent = tangent * derivative + fresh
        return (fresh, tangent, weight_var / 2.0 * row_var + bias_var, weight_var / 2.0 * part_var + bias_var)
    start = (base_kernel, base_kernel, q_rows[None, :, None], q_parts[:, None, :])
    return lax.fori_loop(0, LAYERS, one_layer, start)[1]

def reference(data, slot_of_block, pair_rows, partners):

    def device_pairs(blocks):
        row_block, partner_block = blocks
        row_data = data[slot_of_block[row_block]].astype(jnp.float32)
        partner_data = data[slot_of_block[partner_block]].astype(jnp.float32)
        base_kernel = jnp.einsum('id,pjd->pij', row_data, partner_data) / D
        q_rows = lax.optimization_barrier(jnp.sum(row_data * row_data, axis=-1)) / D
        q_parts = lax.optimization_barrier(jnp.sum(partner_data * partner_data, axis=-1)) / D
        return recurse(base_kernel, q_rows, q_parts)
    tiles = lax.map(device_pairs, (pair_rows.reshape(-1), partners.reshape(-1, PAIRS_DEV)))
    return tiles.reshape(N_ROW, N_COL, PAIRS_DEV, BLK, BLK)
```

```python
import functools

import jax
import jax.numpy as jnp
from jax import lax
from jax.experimental import pallas as pl
from jax.experimental.pallas import tpu as pltpu
from jax.sharding import PartitionSpec as P

LAYERS = 10
CAP = 2
WEIGHT_VAR = 2.0
BIAS_VAR = 0.05
BATCH = 2
DELAY = 2
STEPS = 9
PHASES = (256, 384)


ANY = pl.BlockSpec(memory_space=pl.ANY)
SMEM = pl.BlockSpec(memory_space=pltpu.SMEM)

ACOS = (
    1.5707963050,
    -0.2145988016,
    0.0889789874,
    -0.0501743046,
    0.0308918810,
    -0.0170881256,
    0.0066700901,
    -0.0012624911,
)
PI = 3.14159265358979


def recurse(base_kernel, q_rows, q_parts):
    def one_layer(depth, carry):
        covariance, tangent, row_var, part_var = carry
        slack = jnp.maximum(row_var * part_var - covariance * covariance, 0.0)
        sine_part = jnp.sqrt(slack)
        opening = jnp.arctan2(sine_part, covariance)
        fresh = (
            WEIGHT_VAR / (2.0 * jnp.pi) * (sine_part + (jnp.pi - opening) * covariance) + BIAS_VAR
        )
        derivative = WEIGHT_VAR / (2.0 * jnp.pi) * (jnp.pi - opening)
        tangent = tangent * derivative + fresh
        return (
            fresh,
            tangent,
            WEIGHT_VAR / 2.0 * row_var + BIAS_VAR,
            WEIGHT_VAR / 2.0 * part_var + BIAS_VAR,
        )

    start = (base_kernel, base_kernel, q_rows[None, :, None], q_parts[:, None, :])
    return lax.fori_loop(0, LAYERS, one_layer, start)[1]


def lookup(positions, entries):
    matches = positions[..., None] == jnp.arange(entries.shape[0], dtype=jnp.int32)
    return jnp.sum(jnp.where(matches, entries, 0), axis=-1)


def squares(pieces):
    return jnp.sum(jnp.square(pieces.astype(jnp.float32)), axis=-1)


def padded_exchange(data, slot_of_block, pair_rows, partners):
    row_count = lax.axis_size("row")
    here_row = lax.axis_index("row")
    blocks_here, block_rows, slice_width = data.shape
    features = slice_width * lax.axis_size("col")
    col_count = partners.shape[1]
    pairs_each = partners.shape[2]
    requests = pairs_each * col_count
    storage = lookup(partners.reshape(row_count, requests), slot_of_block)
    owners = storage // blocks_here
    within = storage % blocks_here
    owned_here = (owners == here_row).astype(jnp.int32)
    slot_rank = jnp.cumsum(owned_here, axis=1) - 1
    slot_ids = jnp.arange(CAP, dtype=jnp.int32)
    local_ids = jnp.arange(blocks_here, dtype=jnp.int32)
    selector = (
        (owned_here[:, :, None, None] == 1)
        & (slot_rank[:, :, None, None] == slot_ids[None, None, :, None])
        & (within[:, :, None, None] == local_ids[None, None, None, :])
    )
    selector = jnp.sum(selector.astype(jnp.float32), axis=1).astype(jnp.bfloat16)
    outgoing = jnp.einsum(
        "ksl,lbd->ksbd", selector, data, preferred_element_type=jnp.float32
    ).astype(jnp.bfloat16)
    incoming = lax.all_to_all(outgoing, "row", split_axis=0, concat_axis=0, tiled=True)
    asked_owners = lax.dynamic_index_in_dim(owners, here_row, 0, keepdims=False)
    positions = jnp.arange(requests, dtype=jnp.int32)
    earlier = positions[None, :] < positions[:, None]
    same_owner = asked_owners[None, :] == asked_owners[:, None]
    asked_rank = jnp.sum((earlier & same_owner).astype(jnp.int32), axis=1)
    target_slot = asked_owners * CAP + asked_rank
    chooser = (
        target_slot[:, None] == jnp.arange(row_count * CAP, dtype=jnp.int32)[None, :]
    ).astype(jnp.bfloat16)
    received = incoming.reshape(row_count * CAP, block_rows, slice_width)
    partner_slices = jnp.einsum(
        "qm,mbd->qbd", chooser, received, preferred_element_type=jnp.float32
    ).astype(jnp.bfloat16)
    row_blocks = lax.dynamic_index_in_dim(pair_rows, here_row, 0, keepdims=False)
    row_within = lookup(row_blocks, slot_of_block) % blocks_here
    row_chooser = (row_within[:, None] == local_ids[None, :]).astype(jnp.bfloat16)
    row_slices = jnp.einsum(
        "cl,lbd->cbd", row_chooser, data, preferred_element_type=jnp.float32
    ).astype(jnp.bfloat16)
    grouped = partner_slices.reshape(col_count, pairs_each, block_rows, slice_width)
    product = jnp.einsum("cid,cpjd->cpij", row_slices, grouped, preferred_element_type=jnp.float32)
    summed = lax.psum_scatter(
        product.reshape(requests, block_rows, block_rows), "col", scatter_dimension=0, tiled=True
    )
    row_sq, part_sq = (
        lax.psum_scatter(squares(row_slices), "col", scatter_dimension=0, tiled=True),
        lax.psum_scatter(squares(partner_slices), "col", scatter_dimension=0, tiled=True),
    )
    return recurse(summed / features, row_sq[0] / features, part_sq / features)


def plan_kernel(dims, slots_ref, wanted_ref, here_ref, tab_ref, req, reach, sent, used):
    planes, plane_blocks, local, n_col, pairs, steps = dims
    limit = steps * BATCH
    requests = n_col * pairs
    total = planes * plane_blocks
    here_z, here_x, here_c = here_ref[0], here_ref[1], here_ref[2]

    def clear(i, _):
        reach[0, i] = -1
        reach[1, i] = planes
        return 0

    lax.fori_loop(0, total, clear, 0)

    def clear_tab(i, _):
        tab_ref[i] = 0
        return 0

    lax.fori_loop(0, 2 * limit, clear_tab, 0)

    def note(i, _):
        s = slots_ref[wanted_ref[i]]
        req[i] = s
        home = s // plane_blocks
        goal = i // (2 * requests)

        @pl.when(goal > home)
        def _():
            reach[0, s] = jnp.maximum(reach[0, s], goal)

        @pl.when(goal < home)
        def _():
            reach[1, s] = jnp.minimum(reach[1, s], goal)

        return 0

    lax.fori_loop(0, 2 * planes * requests, note, 0)

    def own_code(s):
        inside = s % plane_blocks
        return jnp.where(inside // local == here_x, 0, local) + inside % local

    last = jnp.int32(0)
    for way in range(2):
        step = 1 if way == 0 else -1
        for link in range(planes - 1):
            at = link if way == 0 else planes - 1 - link

            def free(i, _):
                used[i] = 0
                return 0

            lax.fori_loop(0, limit, free, 0)
            for far in range(planes - 1, link, -1):
                goal = far if way == 0 else planes - 1 - far
                for back in range(link + 1):
                    home = at - step * back

                    def place(i, last):
                        s = home * plane_blocks + i

                        def put(last):
                            ready = 0
                            if back > 0:
                                ready = (sent[way, at - step, s] // BATCH + DELAY) * BATCH
                            t = lax.while_loop(
                                lambda t: (t < limit) & (used[jnp.minimum(t, limit - 1)] == 1),
                                lambda t: t + 1,
                                jnp.minimum(jnp.int32(ready), limit),
                            )
                            sent[way, at, s] = t

                            @pl.when(t < limit)
                            def _():
                                used[t] = 1

                                @pl.when(at == here_z)
                                def _():
                                    code = own_code(s)
                                    if back > 0:
                                        code = 2 * local + way * limit + sent[way, at - step, s]
                                    tab_ref[way * limit + t] = code

                            return jnp.maximum(last, t + 1)

                        return lax.cond(reach[way, s] == goal, put, lambda last: last, last)

                    last = lax.fori_loop(0, plane_blocks, place, last)
    for dx in range(2):
        for dc in range(n_col):
            for p in range(pairs):
                row = here_z * 2 + jnp.bitwise_xor(here_x, dx)
                s = req[row * requests + jnp.bitwise_xor(here_c, dc) * pairs + p]
                home = s // plane_blocks
                below = sent[0, jnp.maximum(here_z - 1, 0), s]
                above = sent[1, jnp.minimum(here_z + 1, planes - 1), s]
                code = jnp.where(
                    home == here_z,
                    own_code(s),
                    2 * local
                    + jnp.where(
                        home < here_z,
                        jnp.minimum(below, limit - 1),
                        limit + jnp.minimum(above, limit - 1),
                    ),
                )
                tab_ref[2 * limit + (dx * n_col + dc) * pairs + p] = code
    tab_ref[2 * limit + 2 * n_col * pairs] = last


def make_plan(slot_of_block, partners, here, local, steps):
    n_row, n_col, pairs = partners.shape
    planes, plane_blocks = n_row // 2, 2 * local
    dims = (planes, plane_blocks, local, n_col, pairs, steps)
    size = 2 * steps * BATCH + 2 * n_col * pairs + 1
    return pl.pallas_call(
        functools.partial(plan_kernel, dims),
        out_shape=jax.ShapeDtypeStruct((size,), jnp.int32),
        in_specs=[SMEM] * 3,
        out_specs=SMEM,
        scratch_shapes=[
            pltpu.SMEM((n_row * n_col * pairs,), jnp.int32),
            pltpu.SMEM((2, planes * plane_blocks), jnp.int32),
            pltpu.SMEM((2, planes, planes * plane_blocks), jnp.int32),
            pltpu.SMEM((steps * BATCH,), jnp.int32),
        ],
        name="plan",
    )(slot_of_block, partners.reshape(-1), here)


def gather_kernel(entries, groups, local, limit, half, first, n_out, tab_ref, here_ref, data_ref,
                  cross_ref, *rest):
    n_in = len(groups)
    recv = rest[:n_in]
    outs = rest[n_in:n_in + n_out]
    stage, in_sem, out_sem = rest[n_in + n_out:]
    offset = pl.multiple_of(first + here_ref[1] * half, 16)
    for e, (place, _, _, ways) in enumerate(entries):
        code = tab_ref[place]

        @pl.when(code < local)
        def _():
            pltpu.make_async_copy(
                data_ref.at[code, pl.ds(offset, half)], stage.at[e], in_sem.at[e]
            ).start()

        @pl.when((code >= local) & (code < 2 * local))
        def _():
            pltpu.make_async_copy(cross_ref.at[code - local], stage.at[e], in_sem.at[e]).start()

        for (way, number), ref in zip(groups, recv):
            if way not in ways:
                continue
            low = 2 * local + way * limit + number * BATCH

            @pl.when((code >= low) & (code < low + BATCH))
            def _():
                pltpu.make_async_copy(ref.at[code - low], stage.at[e], in_sem.at[e]).start()

    for e, (_, out, index, _) in enumerate(entries):
        pltpu.make_async_copy(cross_ref.at[0], stage.at[e], in_sem.at[e]).wait()
        pltpu.make_async_copy(stage.at[e], outs[out].at[index], out_sem.at[e]).start()
    for e, (_, out, index, _) in enumerate(entries):
        pltpu.make_async_copy(stage.at[e], outs[out].at[index], out_sem.at[e]).wait()


def gather(tab, here, data, cross, recv, entries, outs, limit, first, name):
    local, _, width = data.shape
    half = cross.shape[1]
    groups = tuple(sorted(recv))
    moved = 2 * len(entries) * half * width * 2
    return pl.pallas_call(
        functools.partial(
            gather_kernel, entries, groups, local, limit, half, first, len(outs)
        ),
        out_shape=[jax.ShapeDtypeStruct((n, half, width), data.dtype) for n in outs],
        in_specs=[SMEM, SMEM] + [ANY] * (2 + len(groups)),
        out_specs=[ANY] * len(outs),
        scratch_shapes=[
            pltpu.VMEM((len(entries), half, width), data.dtype),
            pltpu.SemaphoreType.DMA((len(entries),)),
            pltpu.SemaphoreType.DMA((len(entries),)),
        ],
        compiler_params=pltpu.CompilerParams(vmem_limit_bytes=len(entries) * half * width * 2 + (2 << 20)),
        cost_estimate=pl.CostEstimate(flops=0, transcendentals=0, bytes_accessed=moved),
        name=name,
    )(tab, here, data, cross, *[recv[g] for g in groups])


def layers(k, a, b):
    tangent = k
    for depth in range(LAYERS):
        both = a * b
        inverse = lax.rsqrt(jnp.maximum(both, 1e-36))
        cosine = k * inverse
        near = jnp.abs(cosine) if depth == 0 else cosine
        gap = jnp.maximum(1.0 - near, 1e-30)
        root = gap * lax.rsqrt(gap)
        poly = jnp.full_like(k, ACOS[-1] / PI)
        for coefficient in ACOS[-2::-1]:
            poly = poly * near + coefficient / PI
        angle = root * poly
        share = 1.0 - angle
        if depth == 0:
            share = jnp.where(cosine < 0.0, angle, share)
        slack = jnp.maximum(both - k * k, 1e-36)
        sine = slack * lax.rsqrt(slack)
        k = share * k + (sine * (WEIGHT_VAR / (2.0 * PI)) + BIAS_VAR)
        tangent = tangent * share + k
        a = a + BIAS_VAR
        b = b + BIAS_VAR
    return tangent


TILE = 64


def tile_kernel(n_col, pairs, half, first, has_old, *refs):
    here_ref = refs[0]
    row_refs = refs[1:1 + n_col]
    row_var_ref = refs[1 + n_col]
    part_refs = refs[2 + n_col:2 + 3 * n_col]
    out_ref = refs[2 + 3 * n_col + has_old]
    rows_v, parts_v, var_v, qpart, kbuf, obuf, row_sem, part_sem, var_sem, out_sem = refs[
        3 + 3 * n_col + has_old:
    ]
    x = here_ref[1]
    size = 2 * half
    block_rows, width = row_refs[0].shape
    features = n_col * width

    def copies():
        for c in range(n_col):
            yield pltpu.make_async_copy(row_refs[c], rows_v.at[c], row_sem.at[c])
        yield pltpu.make_async_copy(row_var_ref, var_v, var_sem)
        for dx in range(2):
            at = pl.multiple_of(jnp.bitwise_xor(x, dx) * half, 16)
            for c in range(n_col):
                for p in range(pairs):
                    yield pltpu.make_async_copy(
                        part_refs[dx * n_col + c].at[p],
                        parts_v.at[p, c, pl.ds(at, half)],
                        part_sem.at[dx, c, p],
                    )

    for copy in copies():
        copy.start()
    for copy in copies():
        copy.wait()

    for p in range(pairs):
        for j in range(size // 128):
            total = jnp.zeros((128, 128), jnp.float32)
            for c in range(n_col):
                for w in range(width // 128):
                    piece = parts_v[p, c, pl.ds(j * 128, 128), pl.ds(w * 128, 128)].astype(jnp.float32)
                    total = total + piece * piece
            qpart[p, :, pl.ds(j * 128, 128)] = jnp.broadcast_to(
                jnp.sum(total.T, axis=0, keepdims=True) / features, (8, 128)
            )

        def some_rows(i, _):
            r = pl.multiple_of(i * 128, 128)
            for j in range(size // 128):
                acc = jnp.zeros((128, 128), jnp.float32)
                for c in range(n_col):
                    acc = acc + lax.dot_general(
                        rows_v[c, pl.ds(r, 128), :],
                        parts_v[p, c, pl.ds(j * 128, 128), :],
                        (((1,), (1,)), ((), ())),
                        preferred_element_type=jnp.float32,
                    )
                kbuf[:, pl.ds(j * 128, 128)] = acc * (1.0 / features)

            def one(u, _):
                top = pl.multiple_of((u % (128 // TILE)) * TILE, TILE)
                left = pl.multiple_of((u // (128 // TILE)) * 128, 128)
                k = kbuf[pl.ds(top, TILE), pl.ds(left, 128)]
                a = var_v[pl.ds(pl.multiple_of(r + top, TILE), TILE), :]
                b = qpart[p, pl.ds(0, 1), pl.ds(left, 128)]
                obuf[p, pl.ds(pl.multiple_of(r + top, TILE), TILE), pl.ds(left, 128)] = layers(
                    k, a, jnp.broadcast_to(b, (TILE, 128))
                )
                return 0

            lax.fori_loop(0, (size // 128) * (128 // TILE), one, 0)
            return 0

        lax.fori_loop(0, block_rows // 128, some_rows, 0)
        pltpu.make_async_copy(
            obuf.at[p], out_ref.at[p, :, pl.ds(first, size)], out_sem.at[p]
        ).start()
    for p in range(pairs):
        pltpu.make_async_copy(
            obuf.at[p], out_ref.at[p, :, pl.ds(first, size)], out_sem.at[p]
        ).wait()


def tiles(here, row_slices, row_var, parts, first, old):
    n_col = len(row_slices)
    block_rows, width = row_slices[0].shape
    pairs, half, _ = parts[0].shape
    size = 2 * half
    has_old = old is not None
    flops = 2 * pairs * block_rows * size * width * n_col
    moved = (n_col * block_rows * width + 2 * n_col * pairs * half * width) * 2 + pairs * block_rows * size * 4
    n_in = 2 + 3 * n_col
    out_shape = jax.ShapeDtypeStruct((pairs, block_rows, block_rows), jnp.float32)
    return pl.pallas_call(
        functools.partial(tile_kernel, n_col, pairs, half, first, has_old),
        out_shape=out_shape,
        in_specs=[SMEM] + [ANY] * (n_in - 1 + has_old),
        out_specs=ANY,
        input_output_aliases={n_in: 0} if has_old else {},
        scratch_shapes=[
            pltpu.VMEM((n_col, block_rows, width), jnp.bfloat16),
            pltpu.VMEM((pairs, n_col, size, width), jnp.bfloat16),
            pltpu.VMEM((block_rows, 128), jnp.float32),
            pltpu.VMEM((pairs, 8, size), jnp.float32),
            pltpu.VMEM((128, size), jnp.float32),
            pltpu.VMEM((pairs, block_rows, size), jnp.float32),
            pltpu.SemaphoreType.DMA((n_col,)),
            pltpu.SemaphoreType.DMA((2, n_col, pairs)),
            pltpu.SemaphoreType.DMA,
            pltpu.SemaphoreType.DMA((pairs,)),
        ],
        compiler_params=pltpu.CompilerParams(vmem_limit_bytes=32 << 20),
        cost_estimate=pl.CostEstimate(
            flops=flops, transcendentals=3 * LAYERS * pairs * block_rows * size, bytes_accessed=moved
        ),
        name="tiles",
    )(here, *row_slices, row_var, *parts, *([old] if has_old else []))


def on_device(n_row, n_col, data, slot_of_block, pair_rows, partners):
    local, block_rows, width = data.shape
    pairs = partners.shape[2]
    planes = n_row // 2
    me_r, me_c = lax.axis_index("row"), lax.axis_index("col")
    z, x = me_r // 2, me_r % 2
    here = jnp.stack([z, x, me_c]).astype(jnp.int32)
    limit = STEPS * BATCH
    tab = make_plan(slot_of_block, partners, here, local, STEPS)

    def flip(value, dx, dc):
        if dx == 0 and dc == 0:
            return value
        moves = [
            (r * n_col + c, (r ^ dx) * n_col + (c ^ dc)) for r in range(n_row) for c in range(n_col)
        ]
        return lax.ppermute(value, ("row", "col"), moves)

    up = [(r, r + 2) for r in range(n_row - 2)]
    down = [(r + 2, r) for r in range(n_row - 2)]

    cross = []
    first = 0
    for size in PHASES:
        half = size // 2
        mine = lax.dynamic_slice(
            data, (0, first + (1 - x) * half, 0), (local, half, width)
        )
        cross.append(flip(mine, 1, 0))
        first += size

    row_blocks = lax.dynamic_index_in_dim(pair_rows, me_r, 0, keepdims=False)
    row_within = lookup(row_blocks, slot_of_block) % local
    row_slices = []
    for dc in range(n_col):
        goal = jnp.bitwise_xor(me_c, dc)
        which = jnp.sum(jnp.where(jnp.arange(n_col) == goal, row_within, 0))
        row_slices.append(
            flip(lax.dynamic_index_in_dim(data, which, 0, keepdims=False), 0, dc)
        )
    row_var = sum(squares(piece) for piece in row_slices) / (n_col * width)
    row_var = jnp.broadcast_to(row_var[:, None], (block_rows, 128))

    result = None
    first = 0
    for phase, size in enumerate(PHASES):
        recv = {}
        for t in range(STEPS):
            known = {g: v for g, v in recv.items() if g[1] <= t - DELAY}
            entries = [
                (way * limit + t * BATCH + i, way, i, (way,)) for way in range(2) for i in range(BATCH)
            ]
            sends = gather(
                tab, here, data, cross[phase], known, entries, (BATCH, BATCH), limit, first,
                f"pick{phase}_{t}",
            )
            recv[0, t] = lax.ppermute(sends[0], "row", up)
            recv[1, t] = lax.ppermute(sends[1], "row", down)
        entries = [
            (2 * limit + m * pairs + p, m, p, (0, 1)) for m in range(2 * n_col) for p in range(pairs)
        ]
        out = gather(
            tab, here, data, cross[phase], recv, entries, (pairs,) * (2 * n_col), limit, first,
            f"deliver{phase}",
        )
        parts = [flip(out[dx * n_col + dc], dx, dc) for dx in range(2) for dc in range(n_col)]
        result = tiles(here, row_slices, row_var, parts, first, result)
        first += size

    fits = tab[2 * limit + 2 * n_col * pairs] <= limit
    result = lax.cond(
        fits,
        lambda *_: result,
        lambda *args: padded_exchange(*args),
        data, slot_of_block, pair_rows, partners,
    )
    return result[None, None]


def solution(mesh):
    return jax.shard_map(
        functools.partial(on_device, mesh.shape["row"], mesh.shape["col"]),
        mesh=mesh,
        in_specs=(P("row", None, "col"), P(), P(), P()),
        out_specs=P("row", "col", None, None, None),
        check_vma=False,
    )
```
